32 devices in a mesh: ctx: 8 (over z, y), head: 4 (over x, core).
Axes of the slice: x: 2, y: 2, z: 4, core: 2. Of those that a mesh axis runs over, the one named last changes fastest.
Arguments:
- query_rows: bfloat16 [8192, 4096], P('ctx', 'head'), may hold values from -6 to 6
- key_rows: bfloat16 [8192, 4096], P('ctx', 'head'), may hold values from -6 to 6
- value_rows: bfloat16 [8192, 4096], P('ctx', 'head'), may hold values from -6 to 6
- level_gate: float32 [6, 32, 8192], P(None, 'head', 'ctx'), may hold values from 0 to 2.5, as said below
- out_weight: bfloat16 [4096, 4096], P('head'), may hold values from -0.09375 to 0.09375
Outputs:
- output: bfloat16 [8192, 4096], P(('ctx', 'head'))
The draws below stay inside these ranges and needn't reach their ends.
Inputs may be any that keep to these rules, and one draw needn't show every extreme that they name: `level_gate`: every gate weight is positive.
All inputs are finite; a program needn't handle non-finite values.
Results may differ from the reference program's by a relative error of at most 0.015.
Values may be sent and summed in bfloat16 or wider, within the bound.
A program may use at most 128 MiB of HBM per device.

```python
import math
import jax
import jax.numpy as jnp
from jax import lax

H = 32
DH = 128
D = 4096
C = 256
LEVELS = 6
SEQ = 8192
N_HEAD = 4


def draw_level_gate(key, part):
    level_ids = jnp.arange(LEVELS, dtype=jnp.float32)[:, None, None]
    base_gate = jnp.exp(jax.random.uniform(key, (LEVELS, H, SEQ), jnp.float32, math.log(0.25), math.log(2.5)))
    return base_gate * jnp.exp(-0.5 * math.log(2.0) * level_ids)


def levels(own_key, dims, pieces, least, high):
    loudness, own = 1.0, jax.random.fold_in(own_key, 6)
    for position, shards_of in pieces:
        steps = jnp.exp(jax.random.uniform(jax.random.fold_in(own, position), (shards_of,), jnp.float32, least / len(pieces), high / len(pieces)))
        loudness = loudness * jnp.repeat(steps, dims[position] // shards_of).reshape([-1 if axis == position else 1 for axis in range(len(dims))])
    return loudness


def scatter_about(key, extent, width, limit, pieces=(), kind=jnp.bfloat16):
    entries = width * jax.random.normal(key, extent, jnp.float32)
    if pieces:
        entries = entries * levels(key, extent, pieces, -0.22, 0.18)
    return jnp.clip(entries, -limit, limit).astype(kind)


def setup_inputs(seed: int = 0) -> dict:
    seeds = jax.random.split(jax.random.key(seed), 6)
    query_rows = scatter_about(seeds[0], (SEQ, H * DH), 1.0, 6.0, ((0, 8), (1, 4)))
    key_rows = scatter_about(seeds[1], (SEQ, H * DH), 1.0, 6.0, ((0, 8), (1, 4)))
    value_rows = scatter_about(seeds[2], (SEQ, H * DH), 1.0, 6.0, ((0, 8), (1, 4)))
    level_gate = draw_level_gate(jax.random.fold_in(seeds[5], 71), 0)
    out_weight = scatter_about(seeds[4], (H * DH, D), (H * DH) ** -0.5, 0.09375, ((0, 4),))
    return {"query_rows": query_rows, "key_rows": key_rows, "value_rows": value_rows, "level_gate": level_gate, "out_weight": out_weight}


EPS = 1e-06

def head_block(query_rows, key_rows, value_rows, level_gate, head_id):
    seq_len = query_rows.shape[0]
    num_stretches = seq_len // C
    col_start = (head_id * DH).astype(jnp.int32)
    query_stretches = lax.dynamic_slice_in_dim(query_rows, col_start, DH, 1).reshape(num_stretches, C, DH).astype(jnp.float32)
    key_stretches = lax.dynamic_slice_in_dim(key_rows, col_start, DH, 1).reshape(num_stretches, C, DH).astype(jnp.float32)
    value_stretches = lax.dynamic_slice_in_dim(value_rows, col_start, DH, 1).reshape(num_stretches, C, DH).astype(jnp.float32)
    gates = lax.dynamic_slice_in_dim(level_gate, head_id.astype(jnp.int32), 1, 1)[:, 0, :].reshape(LEVELS, num_stretches, C)
    scores = jnp.einsum('cti,csi->cts', query_stretches, key_stretches)
    row_ids = lax.broadcasted_iota(jnp.int32, (C, C), 0)
    col_ids = lax.broadcasted_iota(jnp.int32, (C, C), 1)
    weights = (jnp.where(row_ids >= col_ids, scores, 0.0) * gates[0][:, :, None]).astype(jnp.bfloat16)
    combined = jnp.einsum('cts,csj->ctj', weights.astype(jnp.float32), value_stretches)
    stretch_state = jnp.einsum('csi,csj->cij', key_stretches, value_stretches)
    stretch_ids = jnp.arange(num_stretches, dtype=jnp.int32)
    for level_bit in range(LEVELS - 1):
        span_size = 2 ** level_bit
        grouped = stretch_state.reshape(num_stretches // span_size, span_size, DH, DH).sum(axis=1)
        owner_block = stretch_ids // span_size
        bucket = grouped[jnp.maximum(owner_block - 1, 0)].astype(jnp.bfloat16)
        readout = jnp.einsum('cti,cij->ctj', query_stretches, bucket.astype(jnp.float32))
        combined = combined + jnp.where((owner_block % 2 == 1)[:, None, None], readout * gates[level_bit + 1][:, :, None], 0.0)
    normed = combined * lax.rsqrt(lax.optimization_barrier(jnp.mean(combined * combined, axis=-1, keepdims=True)) + EPS)
    return normed.astype(jnp.bfloat16).reshape(seq_len, DH)

def reference(query_rows, key_rows, value_rows, level_gate, out_weight):
    head_ids = jnp.arange(H, dtype=jnp.int32)
    blocks = lax.map(lambda head_id: head_block(query_rows, key_rows, value_rows, level_gate, head_id), head_ids)
    seq_len = query_rows.shape[0]
    normed = jnp.transpose(blocks, (1, 0, 2)).reshape(seq_len, H * DH)
    group_cols = H // N_HEAD * DH
    result = jnp.zeros((seq_len, D), jnp.float32)
    for group_index in range(N_HEAD):
        lower = group_index * group_cols
        upper = lower + group_cols
        partial_value = jnp.dot(normed[:, lower:upper], out_weight[lower:upper], preferred_element_type=jnp.float32)
        partial_value = lax.optimization_barrier(partial_value.astype(jnp.bfloat16)).astype(jnp.float32)
        result = result + partial_value
    return result.astype(jnp.bfloat16)
```

```python
import functools

import jax
import jax.numpy as jnp
from jax import lax
from jax.experimental import pallas as pl
from jax.experimental.pallas import tpu as pltpu
from jax.sharding import PartitionSpec as P

C = 256
EPS = 1e-06
CHUNKS = 4
TILE = 512
MESH = pl.DeviceIdType.MESH
F32 = jnp.float32
BF16 = jnp.bfloat16


def buckets_of(stretches):
    keys = []
    span = 1
    while span < stretches:
        keys += [(span, block) for block in range(0, stretches // span, 2)]
        span *= 2
    return keys


def kernel(
    ctx_bits, heads, levels,
    q_hbm, k_hbm, v_hbm, g_hbm, w_hbm, out_hbm,
    q, k, v, g, gate_cols, w, comb, run, near, s_buf, r_buf,
    to_sib, from_sib, mine, p_send, p_recv, own, o_buf,
    load_sem, st_send, st_recv, w_send, w_recv, n_send, n_recv, p_ssem, p_rsem, o_sem,
):
    tokens, width = q.shape[0], q.shape[1] // heads
    stretches = tokens // C
    bits = stretches.bit_length() - 1
    per = heads // CHUNKS
    rows = own.shape[0]
    tiles = p_send.shape[0]
    keys = buckets_of(stretches)
    me = lax.axis_index("ctx")
    head_at = lax.axis_index("head")
    digits = [lax.rem(lax.div(me, 2**b), 2) for b in range(ctx_bits)]
    partners = [{"ctx": me + (1 - 2 * digits[b]) * 2**b} for b in range(ctx_bits)]
    core = lax.rem(head_at, 2)
    pair = lax.div(head_at, 2)
    sib = {"head": pair * 2 + 1 - core}
    far_dev = {"head": (1 - pair) * 2 + core}

    loads = [
        pltpu.make_async_copy(src, dst, load_sem.at[n])
        for n, (src, dst) in enumerate(
            ((k_hbm, k), (v_hbm, v), (q_hbm, q), (g_hbm, g), (w_hbm, w.at[0]))
        )
    ]
    for copy in loads:
        copy.start()

    barrier = pltpu.get_barrier_semaphore()
    everyone = partners + [sib, far_dev]
    for device in everyone:
        pl.semaphore_signal(barrier, inc=1, device_id=device, device_id_type=MESH)
    pl.semaphore_wait(barrier, len(everyone))

    w_copy = pltpu.make_async_remote_copy(
        src_ref=w_hbm, dst_ref=w.at[1], send_sem=w_send, recv_sem=w_recv,
        device_id=sib, device_id_type=MESH,
    )
    w_copy.start()

    def state_copy(level, chunk):
        part = pl.ds(chunk * per, per)
        return pltpu.make_async_remote_copy(
            src_ref=s_buf.at[level, part], dst_ref=r_buf.at[level, part],
            send_sem=st_send.at[level, chunk], recv_sem=st_recv.at[level, chunk],
            device_id=partners[level], device_id_type=MESH,
        )

    def service(level, chunk):
        state_copy(level, chunk).wait_recv()
        if level + 1 < ctx_bits:
            part = pl.ds(chunk * per, per)
            total = run[part] + r_buf[level, part].astype(F32)
            run[part] = total
            s_buf[level + 1, part] = total.astype(BF16)
            state_copy(level + 1, chunk).start()

    def lanes(head):
        return pl.ds(pl.multiple_of(head * width, width), width)

    loads[0].wait()
    loads[1].wait()

    @pl.loop(0, CHUNKS)
    def _(chunk):
        for inner in range(per):
            head = chunk * per + inner
            col = lanes(head)
            sums = {}
            for c in range(stretches):
                token = pl.ds(c * C, C)
                sums[1, c] = lax.dot_general(
                    k[token, col], v[token, col], (((0,), (0,)), ((), ())),
                    preferred_element_type=F32,
                )
            span = 1
            while span < stretches:
                for block in range(stretches // span // 2):
                    sums[span * 2, block] = sums[span, block * 2] + sums[span, block * 2 + 1]
                span *= 2
            for n, key in enumerate(keys):
                near[head, n] = sums[key].astype(BF16)
            run[head] = sums[stretches, 0]
            s_buf[0, head] = sums[stretches, 0].astype(BF16)
        state_copy(0, chunk).start()

    loads[2].wait()
    loads[3].wait()
    pad = gate_cols.shape[2] - levels
    for head in range(heads):
        strips = [g[level, head : head + 1, :] for level in range(levels)]
        if pad:
            strips.append(jnp.zeros((pad, tokens), F32))
        gate_cols[head] = jnp.concatenate(strips, axis=0).T

    keep = lax.broadcasted_iota(jnp.int32, (C, C), 0) >= lax.broadcasted_iota(
        jnp.int32, (C, C), 1
    )

    @pl.loop(0, CHUNKS)
    def _(chunk):
        for inner in range(per):
            head = chunk * per + inner
            col = lanes(head)
            for c in range(stretches):
                token = pl.ds(c * C, C)
                gates = gate_cols[head, token, :]
                query = q[token, col]
                scores = lax.dot_general(
                    query, k[token, col], (((1,), (1,)), ((), ())), preferred_element_type=F32
                )
                weights = (jnp.where(keep, scores, 0.0) * gates[:, 0:1]).astype(BF16)
                total = jnp.dot(weights, v[token, col], preferred_element_type=F32)
                for b in range(bits):
                    block = c // 2**b
                    if block % 2:
                        read = jnp.dot(
                            query, near[head, keys.index((2**b, block - 1))],
                            preferred_element_type=F32,
                        )
                        total = total + read * gates[:, b + 1 : b + 2]
                comb[token, col] = total
        for level in range(ctx_bits - 1):
            if level == 0:
                service(0, chunk)
            else:
                @pl.when(chunk >= level)
                def _():
                    service(level, chunk - level)

    for step in range(CHUNKS, CHUNKS + ctx_bits - 2):
        for level in range(1, ctx_bits - 1):
            if 0 <= step - level < CHUNKS:
                service(level, step - level)

    for chunk in range(CHUNKS):
        service(ctx_bits - 1, chunk)

    scale = [digit.astype(F32) for digit in digits]

    def finish(block, dst):
        token = pl.ds(pl.multiple_of(block * rows, rows), rows)

        @pl.loop(0, heads // 2)
        def _(half):
            for inner in range(2):
                head = half * 2 + inner
                col = lanes(head)
                gates = gate_cols[head, token, :]
                query = q[token, col]
                total = comb[token, col]
                for level in range(ctx_bits):
                    read = jnp.dot(query, r_buf[level, head], preferred_element_type=F32)
                    at = bits + 1 + level
                    total = total + read * (gates[:, at : at + 1] * scale[level])
                mean = jnp.mean(total * total, axis=-1, keepdims=True)
                dst[:, col] = (total * lax.rsqrt(mean + EPS)).astype(BF16)

    def sib_copy(n):
        return pltpu.make_async_remote_copy(
            src_ref=to_sib.at[n], dst_ref=from_sib.at[n],
            send_sem=n_send.at[n], recv_sem=n_recv.at[n],
            device_id=sib, device_id_type=MESH,
        )

    def p_copy(tile):
        return pltpu.make_async_remote_copy(
            src_ref=p_send.at[tile], dst_ref=p_recv.at[tile],
            send_sem=p_ssem.at[tile], recv_sem=p_rsem.at[tile],
            device_id=far_dev, device_id_type=MESH,
        )

    def out_copy(tile):
        at = pl.ds(pl.multiple_of(tile * TILE, TILE), TILE)
        return pltpu.make_async_copy(o_buf.at[:, at], out_hbm.at[:, at], o_sem.at[tile])

    def project(n, tile):
        at = pl.ds(pl.multiple_of(tile * TILE, TILE), TILE)
        return jnp.dot(mine[n], w[0, :, at], preferred_element_type=F32) + jnp.dot(
            from_sib[n], w[1, :, at], preferred_element_type=F32
        )

    other = 1 - pair
    finish(other * 2 + 1 - core, to_sib.at[0])
    sib_copy(0).start()
    finish(other * 2 + core, mine.at[0])
    loads[4].wait()
    w_copy.wait_recv()
    sib_copy(0).wait_recv()

    @pl.loop(0, tiles)
    def _(tile):
        p_send[tile] = project(0, tile).astype(BF16)
        p_copy(tile).start()

    finish(pair * 2 + 1 - core, to_sib.at[1])
    sib_copy(1).start()
    finish(pair * 2 + core, mine.at[1])
    sib_copy(1).wait_recv()

    @pl.loop(0, tiles)
    def _(tile):
        own[:, pl.ds(pl.multiple_of(tile * TILE, TILE), TILE)] = project(1, tile)

    @pl.loop(0, tiles)
    def _(tile):
        at = pl.ds(pl.multiple_of(tile * TILE, TILE), TILE)
        p_copy(tile).wait_recv()
        o_buf[:, at] = (own[:, at] + p_recv[tile].astype(F32)).astype(BF16)
        out_copy(tile).start()

    @pl.loop(0, tiles)
    def _(tile):
        p_copy(tile).wait_send()
        out_copy(tile).wait()

    for n in range(2):
        sib_copy(n).wait_send()
    w_copy.wait_send()

    @pl.loop(0, CHUNKS)
    def _(chunk):
        for level in range(ctx_bits):
            state_copy(level, chunk).wait_send()


def on_device(query_rows, key_rows, value_rows, level_gate, out_weight):
    tokens, cols = query_rows.shape
    levels, heads, _ = level_gate.shape
    width = cols // heads
    model = out_weight.shape[1]
    rows = tokens // lax.axis_size("head")
    ctx_bits = lax.axis_size("ctx").bit_length() - 1
    tiles = model // TILE
    near = len(buckets_of(tokens // C))
    dma = pltpu.SemaphoreType.DMA
    flops = 2 * tokens * cols * (model + 2 * C + width * 7)
    return pl.pallas_call(
        functools.partial(kernel, ctx_bits, heads, levels),
        out_shape=jax.ShapeDtypeStruct((rows, model), BF16),
        in_specs=[pl.BlockSpec(memory_space=pl.ANY)] * 5,
        out_specs=pl.BlockSpec(memory_space=pl.ANY),
        scratch_shapes=[
            pltpu.VMEM((tokens, cols), BF16),
            pltpu.VMEM((tokens, cols), BF16),
            pltpu.VMEM((tokens, cols), BF16),
            pltpu.VMEM((levels, heads, tokens), F32),
            pltpu.VMEM((heads, tokens, -(-levels // 8) * 8), F32),
            pltpu.VMEM((2, cols, model), BF16),
            pltpu.VMEM((tokens, cols), F32),
            pltpu.VMEM((heads, width, width), F32),
            pltpu.VMEM((heads, near, width, width), BF16),
            pltpu.VMEM((ctx_bits, heads, width, width), BF16),
            pltpu.VMEM((ctx_bits, heads, width, width), BF16),
            pltpu.VMEM((2, rows, cols), BF16),
            pltpu.VMEM((2, rows, cols), BF16),
            pltpu.VMEM((2, rows, cols), BF16),
            pltpu.VMEM((tiles, rows, TILE), BF16),
            pltpu.VMEM((tiles, rows, TILE), BF16),
            pltpu.VMEM((rows, model), F32),
            pltpu.VMEM((rows, model), BF16),
            dma((5,)),
            dma((ctx_bits, CHUNKS)),
            dma((ctx_bits, CHUNKS)),
            dma(()),
            dma(()),
            dma((2,)),
            dma((2,)),
            dma((tiles,)),
            dma((tiles,)),
            dma((tiles,)),
        ],
        compiler_params=pltpu.CompilerParams(
            collective_id=0, has_side_effects=True, vmem_limit_bytes=64 * 1024 * 1024 - 65536
        ),
        cost_estimate=pl.CostEstimate(
            flops=flops, bytes_accessed=20 * 1024 * 1024, transcendentals=tokens * heads
        ),
        name="levels_project",
    )(query_rows, key_rows, value_rows, level_gate, out_weight)


def solution(mesh):
    in_specs = (
        P("ctx", "head"),
        P("ctx", "head"),
        P("ctx", "head"),
        P(None, "head", "ctx"),
        P("head", None),
    )
    out_specs = P(("ctx", "head"), None)
    return jax.shard_map(
        on_device, mesh=mesh, in_specs=in_specs, out_specs=out_specs, check_vma=False
    )
```

```python
import functools

import jax
import jax.numpy as jnp
from jax import lax
from jax.experimental import pallas as pl
from jax.experimental.pallas import tpu as pltpu
from jax.sharding import PartitionSpec as P

C = 256
EPS = 1e-06
CHUNKS = 4
TILE = 512
MESH = pl.DeviceIdType.MESH
F32 = jnp.float32
BF16 = jnp.bfloat16


def buckets_of(stretches):
    keys = []
    span = 1
    while span < stretches:
        keys += [(span, block) for block in range(0, stretches // span, 2)]
        span *= 2
    return keys


def kernel(
    ctx_bits, heads, levels,
    q_hbm, k_hbm, v_hbm, g_hbm, w_hbm, out_hbm,
    q, k, v, g, gate_cols, w, comb, run, near, s_buf, r_buf,
    to_sib, from_sib, mine, p_send, p_recv, own, o_buf,
    load_sem, st_send, st_recv, hand_send, w_send, w_recv, n_send, n_recv, p_ssem, p_rsem, o_sem,
):
    tokens, width = q.shape[0], q.shape[1] // heads
    stretches = tokens // C
    bits = stretches.bit_length() - 1
    per = heads // CHUNKS
    rows = own.shape[0]
    tiles = p_send.shape[0]
    keys = buckets_of(stretches)
    me = lax.axis_index("ctx")
    head_at = lax.axis_index("head")
    digits = [lax.rem(lax.div(me, 2**b), 2) for b in range(ctx_bits)]
    partners = [{"ctx": me + (1 - 2 * digits[b]) * 2**b} for b in range(ctx_bits)]
    core = lax.rem(head_at, 2)
    pair = lax.div(head_at, 2)
    sib = {"head": pair * 2 + 1 - core}
    far_dev = {"head": (1 - pair) * 2 + core}

    loads = [
        pltpu.make_async_copy(src, dst, load_sem.at[n])
        for n, (src, dst) in enumerate(
            ((k_hbm, k), (v_hbm, v), (q_hbm, q), (g_hbm, g), (w_hbm, w.at[0]))
        )
    ]
    for copy in loads[:4]:
        copy.start()

    barrier = pltpu.get_barrier_semaphore()
    everyone = partners + [sib, far_dev]
    for device in everyone:
        pl.semaphore_signal(barrier, inc=1, device_id=device, device_id_type=MESH)
    pl.semaphore_wait(barrier, len(everyone))

    def w_copy(tile):
        at = pl.ds(pl.multiple_of(tile * TILE, TILE), TILE)
        return pltpu.make_async_remote_copy(
            src_ref=w_hbm.at[:, at], dst_ref=w.at[1, :, at],
            send_sem=w_send.at[tile], recv_sem=w_recv.at[tile],
            device_id=sib, device_id_type=MESH,
        )

    def state_copy(level, chunk):
        part = pl.ds(chunk * per, per)
        return pltpu.make_async_remote_copy(
            src_ref=s_buf.at[level, part], dst_ref=r_buf.at[level, part],
            send_sem=st_send.at[level, chunk], recv_sem=st_recv.at[level, chunk],
            device_id=partners[level], device_id_type=MESH,
        )

    last = ctx_bits - 1

    def hand_copy(chunk):
        part = pl.ds(chunk * per, per)
        return pltpu.make_async_remote_copy(
            src_ref=r_buf.at[last, part], dst_ref=r_buf.at[last, part],
            send_sem=hand_send.at[chunk], recv_sem=st_recv.at[last, chunk],
            device_id=partners[0], device_id_type=MESH,
        )

    def service(level, chunk):
        state_copy(level, chunk).wait_recv()
        if level + 1 < ctx_bits:
            part = pl.ds(chunk * per, per)
            total = run[part] + r_buf[level, part].astype(F32)
            run[part] = total
            s_buf[level + 1, part] = total.astype(BF16)
            if level + 1 < last:
                state_copy(level + 1, chunk).start()
            else:
                @pl.when(chunk % 2 == digits[0])
                def _():
                    state_copy(last, chunk).start()

    def lanes(head):
        return pl.ds(pl.multiple_of(head * width, width), width)

    loads[0].wait()
    loads[1].wait()

    @pl.loop(0, tiles)
    def _(tile):
        w_copy(tile).start()

    loads[4].start()

    @pl.loop(0, CHUNKS)
    def _(chunk):
        for inner in range(per):
            head = chunk * per + inner
            col = lanes(head)
            sums = {}
            for c in range(stretches):
                token = pl.ds(c * C, C)
                sums[1, c] = lax.dot_general(
                    k[token, col], v[token, col], (((0,), (0,)), ((), ())),
                    preferred_element_type=F32,
                )
            span = 1
            while span < stretches:
                for block in range(stretches // span // 2):
                    sums[span * 2, block] = sums[span, block * 2] + sums[span, block * 2 + 1]
                span *= 2
            for n, key in enumerate(keys):
                near[head, n] = sums[key].astype(BF16)
            run[head] = sums[stretches, 0]
            s_buf[0, head] = sums[stretches, 0].astype(BF16)
        state_copy(0, chunk).start()

    loads[2].wait()
    loads[3].wait()
    pad = gate_cols.shape[2] - levels
    for head in range(heads):
        strips = [g[level, head : head + 1, :] for level in range(levels)]
        if pad:
            strips.append(jnp.zeros((pad, tokens), F32))
        gate_cols[head] = jnp.concatenate(strips, axis=0).T

    keep = lax.broadcasted_iota(jnp.int32, (C, C), 0) >= lax.broadcasted_iota(
        jnp.int32, (C, C), 1
    )

    def attend(duo, odd, head):
        block = duo * 2 + odd
        token = pl.ds(pl.multiple_of(block * C, C), C)
        col = lanes(head)
        gates = gate_cols[head, token, :]
        query = q[token, col]
        scores = lax.dot_general(
            query, k[token, col], (((1,), (1,)), ((), ())), preferred_element_type=F32
        )
        weights = (jnp.where(keep, scores, 0.0) * gates[:, 0:1]).astype(BF16)
        total = jnp.dot(weights, v[token, col], preferred_element_type=F32)
        if odd:
            read = jnp.dot(query, near[head, duo], preferred_element_type=F32)
            total = total + read * gates[:, 1:2]
        first = stretches // 2
        for b in range(1, bits):
            span = lax.div(duo, 2 ** (b - 1))
            use = lax.rem(span, 2).astype(F32)
            read = jnp.dot(
                query, near[head, first + lax.div(span, 2)], preferred_element_type=F32
            )
            total = total + read * (gates[:, b + 1 : b + 2] * use)
            first += stretches // 2 ** (b + 1)
        return total

    other = 1 - pair

    @pl.loop(0, CHUNKS)
    def _(chunk):
        for inner in range(per):
            head = chunk * per + inner
            for odd in range(2):
                token = pl.ds(pl.multiple_of((other * 2 + odd) * C, C), C)
                comb[token, lanes(head)] = attend(other, odd, head)
        for level in range(ctx_bits - 1):
            @pl.when((chunk >= level) & (chunk < level + CHUNKS // 2))
            def _():
                for inner in range(2):
                    service(level, (chunk - level) * 2 + inner)

    for step in range(CHUNKS, CHUNKS // 2 + ctx_bits - 2):
        for level in range(ctx_bits - 1):
            if 0 <= step - level < CHUNKS // 2:
                for inner in range(2):
                    service(level, (step - level) * 2 + inner)

    for half in range(CHUNKS // 2):
        chunk = half * 2 + digits[0]
        state_copy(last, chunk).wait_recv()
        hand_copy(chunk).start()
    for half in range(CHUNKS // 2):
        hand_copy(half * 2 + 1 - digits[0]).wait_recv()

    scale = [digit.astype(F32) for digit in digits]

    def finish(block, dst):
        token = pl.ds(pl.multiple_of(block * rows, rows), rows)

        @pl.loop(0, heads // 2)
        def _(half):
            for inner in range(2):
                head = half * 2 + inner
                col = lanes(head)
                gates = gate_cols[head, token, :]
                query = q[token, col]
                total = comb[token, col]
                for level in range(ctx_bits):
                    read = jnp.dot(query, r_buf[level, head], preferred_element_type=F32)
                    at = bits + 1 + level
                    total = total + read * (gates[:, at : at + 1] * scale[level])
                mean = jnp.mean(total * total, axis=-1, keepdims=True)
                dst[:, col] = (total * lax.rsqrt(mean + EPS)).astype(BF16)

    def sib_copy(n):
        return pltpu.make_async_remote_copy(
            src_ref=to_sib.at[n], dst_ref=from_sib.at[n],
            send_sem=n_send.at[n], recv_sem=n_recv.at[n],
            device_id=sib, device_id_type=MESH,
        )

    def p_copy(tile):
        return pltpu.make_async_remote_copy(
            src_ref=p_send.at[tile], dst_ref=p_recv.at[tile],
            send_sem=p_ssem.at[tile], recv_sem=p_rsem.at[tile],
            device_id=far_dev, device_id_type=MESH,
        )

    def out_copy(tile):
        at = pl.ds(pl.multiple_of(tile * TILE, TILE), TILE)
        return pltpu.make_async_copy(o_buf.at[:, at], out_hbm.at[:, at], o_sem.at[tile])

    def project(n, tile):
        at = pl.ds(pl.multiple_of(tile * TILE, TILE), TILE)
        return jnp.dot(mine[n], w[0, :, at], preferred_element_type=F32) + jnp.dot(
            from_sib[n], w[1, :, at], preferred_element_type=F32
        )

    finish(other * 2 + 1 - core, to_sib.at[0])
    sib_copy(0).start()
    finish(other * 2 + core, mine.at[0])
    loads[4].wait()
    sib_copy(0).wait_recv()

    @pl.loop(0, tiles)
    def _(tile):
        w_copy(tile).wait_recv()
        p_send[tile] = project(0, tile).astype(BF16)
        p_copy(tile).start()

    @pl.loop(0, heads)
    def _(head):
        for odd in range(2):
            token = pl.ds(pl.multiple_of((pair * 2 + odd) * C, C), C)
            comb[token, lanes(head)] = attend(pair, odd, head)

    finish(pair * 2 + 1 - core, to_sib.at[1])
    sib_copy(1).start()
    finish(pair * 2 + core, mine.at[1])
    sib_copy(1).wait_recv()

    @pl.loop(0, tiles)
    def _(tile):
        own[:, pl.ds(pl.multiple_of(tile * TILE, TILE), TILE)] = project(1, tile)

    @pl.loop(0, tiles)
    def _(tile):
        at = pl.ds(pl.multiple_of(tile * TILE, TILE), TILE)
        p_copy(tile).wait_recv()
        o_buf[:, at] = (own[:, at] + p_recv[tile].astype(F32)).astype(BF16)
        out_copy(tile).start()

    @pl.loop(0, tiles)
    def _(tile):
        p_copy(tile).wait_send()
        out_copy(tile).wait()
        w_copy(tile).wait_send()

    for n in range(2):
        sib_copy(n).wait_send()

    @pl.loop(0, CHUNKS)
    def _(chunk):
        for level in range(last):
            state_copy(level, chunk).wait_send()

    for half in range(CHUNKS // 2):
        chunk = half * 2 + digits[0]
        state_copy(last, chunk).wait_send()
        hand_copy(chunk).wait_send()


def on_device(query_rows, key_rows, value_rows, level_gate, out_weight):
    tokens, cols = query_rows.shape
    levels, heads, _ = level_gate.shape
    width = cols // heads
    model = out_weight.shape[1]
    rows = tokens // lax.axis_size("head")
    ctx_bits = lax.axis_size("ctx").bit_length() - 1
    tiles = model // TILE
    near = len(buckets_of(tokens // C))
    dma = pltpu.SemaphoreType.DMA
    flops = 2 * tokens * cols * (model + 2 * C + width * 7)
    return pl.pallas_call(
        functools.partial(kernel, ctx_bits, heads, levels),
        out_shape=jax.ShapeDtypeStruct((rows, model), BF16),
        in_specs=[pl.BlockSpec(memory_space=pl.ANY)] * 5,
        out_specs=pl.BlockSpec(memory_space=pl.ANY),
        scratch_shapes=[
            pltpu.VMEM((tokens, cols), BF16),
            pltpu.VMEM((tokens, cols), BF16),
            pltpu.VMEM((tokens, cols), BF16),
            pltpu.VMEM((levels, heads, tokens), F32),
            pltpu.VMEM((heads, tokens, -(-levels // 8) * 8), F32),
            pltpu.VMEM((2, cols, model), BF16),
            pltpu.VMEM((tokens, cols), F32),
            pltpu.VMEM((heads, width, width), F32),
            pltpu.VMEM((heads, near, width, width), BF16),
            pltpu.VMEM((ctx_bits, heads, width, width), BF16),
            pltpu.VMEM((ctx_bits, heads, width, width), BF16),
            pltpu.VMEM((2, rows, cols), BF16),
            pltpu.VMEM((2, rows, cols), BF16),
            pltpu.VMEM((2, rows, cols), BF16),
            pltpu.VMEM((tiles, rows, TILE), BF16),
            pltpu.VMEM((tiles, rows, TILE), BF16),
            pltpu.VMEM((rows, model), F32),
            pltpu.VMEM((rows, model), BF16),
            dma((5,)),
            dma((ctx_bits, CHUNKS)),
            dma((ctx_bits, CHUNKS)),
            dma((CHUNKS,)),
            dma((tiles,)),
            dma((tiles,)),
            dma((2,)),
            dma((2,)),
            dma((tiles,)),
            dma((tiles,)),
            dma((tiles,)),
        ],
        compiler_params=pltpu.CompilerParams(
            collective_id=0, has_side_effects=True, vmem_limit_bytes=64 * 1024 * 1024 - 65536
        ),
        cost_estimate=pl.CostEstimate(
            flops=flops, bytes_accessed=20 * 1024 * 1024, transcendentals=tokens * heads
        ),
        name="levels_project",
    )(query_rows, key_rows, value_rows, level_gate, out_weight)


def solution(mesh):
    in_specs = (
        P("ctx", "head"),
        P("ctx", "head"),
        P("ctx", "head"),
        P(None, "head", "ctx"),
        P("head", None),
    )
    out_specs = P(("ctx", "head"), None)
    return jax.shard_map(
        on_device, mesh=mesh, in_specs=in_specs, out_specs=out_specs, check_vma=False
    )
```
